32 devices in a mesh: tp: 2 (over x), sp: 16 (over z, y, core).
Axes of the slice: x: 2, y: 2, z: 4, core: 2. Of those that a mesh axis runs over, the one named last changes fastest.
Arguments:
- tokens: bfloat16 [2048, 2048], P('sp'), may hold values from -6 to 6
- item_lengths: int32 [4], replicated, may hold values from 128 to 1536, as said below
- first_gain: bfloat16 [2048], replicated, may hold values from 0.25 to 1.75
- query_weight: bfloat16 [2048, 2048], P('tp'), may hold values from -0.125 to 0.125
- key_weight: bfloat16 [1024, 2048], P('tp'), may hold values from -0.125 to 0.125
- value_weight: bfloat16 [1024, 2048], P('tp'), may hold values from -0.125 to 0.125
- headgate_weight: bfloat16 [16, 2048], P('tp'), may hold values from -0.125 to 0.125
- merge_weight: bfloat16 [2048, 2048], P(None, 'tp'), may hold values from -1 to 1
- query_norm: bfloat16 [128], replicated, may hold values from 0.8984375 to 2
- key_norm: bfloat16 [128], replicated, may hold values from 0.8984375 to 2
- second_gain: bfloat16 [2048], replicated, may hold values from 0.25 to 1.75
- gate_weight: bfloat16 [6144, 2048], P(('tp', 'sp')), may hold values from -0.125 to 0.125
- up_weight: bfloat16 [6144, 2048], P(('tp', 'sp')), may hold values from -0.125 to 0.125
- down_weight: bfloat16 [6144, 2048], P(('tp', 'sp')), may hold values from -0.078125 to 0.078125
- out_cotangent: bfloat16 [2048, 2048], P('sp')
Outputs:
- layer_output: bfloat16 [2048, 2048], P('sp')
- input_grad: float32 [2048, 2048], P('sp')
- first_grad: float32 [2048], replicated
- query_grad: float32 [2048, 2048], P('tp')
- key_grad: float32 [1024, 2048], P('tp')
- value_grad: float32 [1024, 2048], P('tp')
- headgate_grad: float32 [16, 2048], P('tp')
- merge_grad: float32 [2048, 2048], P(None, 'tp')
- query_norm_grad: float32 [128], replicated
- key_norm_grad: float32 [128], replicated
- second_grad: float32 [2048], replicated
- gate_grad: float32 [6144, 2048], P(('tp', 'sp'))
- up_grad: float32 [6144, 2048], P(('tp', 'sp'))
- down_grad: float32 [6144, 2048], P(('tp', 'sp'))
The draws below stay inside these ranges and needn't reach their ends.
Inputs may be any that keep to these rules, and one draw needn't show every extreme that they name: `item_lengths`: the item lengths sum to 2048; exactly one item has 1536 tokens, every other at least 128.
All inputs are finite; a program needn't handle non-finite values.
Results may differ from the reference program's by a relative error of at most 0.02.
Values may be sent and summed in bfloat16 or wider, within the bound.
No kernel may reach another device: no remote copies, remote signals or barrier semaphores. Data moves between devices by JAX's collectives and lax.ppermute only.
A program may use at most 384 MiB of HBM per device.

```python
import math
from functools import partial
import jax
import jax.numpy as jnp
from jax import lax

D = 2048
H = 16
KVH = 8
HD = 128
FF = 6144
ITEMS = 4
TOKENS = 2048
LONGEST = 1536


def draw_item_lengths(key, part):
    first_key, second_key = jax.random.split(jax.random.fold_in(key, 11))
    least = TOKENS // 16
    spare = TOKENS - LONGEST - (ITEMS - 1) * least
    cut_points = jnp.sort(jax.random.randint(first_key, (ITEMS - 2,), 0, spare + 1))
    bounds = jnp.concatenate([jnp.zeros((1,), jnp.int32), cut_points.astype(jnp.int32), jnp.full((1,), spare, jnp.int32)])
    others = least + jnp.diff(bounds)
    pieces = jnp.concatenate([jnp.full((1,), LONGEST, jnp.int32), others.astype(jnp.int32)])
    shuffle = jax.random.permutation(second_key, ITEMS)
    return pieces[shuffle].astype(jnp.int32)


def draw_out_cotangent(key, part):
    first_key, second_key = jax.random.split(jax.random.fold_in(key, 23))
    place = jnp.arange(TOKENS, dtype=jnp.float32) / max(TOKENS - 1, 1)
    base = jax.random.normal(first_key, (TOKENS, D), jnp.float32)
    ramp = 0.6 * 3.0 ** place
    rough = jax.random.uniform(second_key, (TOKENS, 1), jnp.float32, 0.7, 1.3)
    return jnp.clip(base * ramp[:, None] * rough, -8.0, 8.0).astype(jnp.bfloat16)


def block_scale(rng, extent, shards, smallest, high):
    def one(dim, blocks):
        heights = jax.random.uniform(jax.random.fold_in(jax.random.fold_in(rng, 6), dim), (blocks,), jnp.float32, smallest / len(shards), high / len(shards))
        return jnp.repeat(jnp.exp(heights), extent[dim] // blocks).reshape((-1,) + (1,) * (len(extent) - dim - 1))

    factor_of = one(*shards[0])
    for cut in shards[1:]:
        factor_of = factor_of * one(*cut)
    return factor_of


def noise(own_key, shape, deviation, most, shards=(), kind=jnp.bfloat16):
    drawn = jax.random.normal(own_key, shape, jnp.float32) * deviation
    if len(shards) > 0:
        drawn = block_scale(own_key, shape, shards, -0.22, 0.18) * drawn
    return jnp.clip(drawn, min=-most, max=most).astype(kind)


def setup_inputs(seed: int = 0) -> dict:
    seeds = jax.random.split(jax.random.key(seed), 16)
    tokens = noise(seeds[0], (TOKENS, D), 1.0, 6.0, ((0, 16),))
    item_lengths = draw_item_lengths(jax.random.fold_in(seeds[15], 71), 0)
    first_gain = jnp.clip(1.0 + 0.15 * jax.random.normal(seeds[2], (D,), jnp.float32), 0.25, 1.75).astype(jnp.bfloat16)
    query_weight = noise(seeds[3], (H * HD, D), D ** -0.5, 0.125, ((0, 2),))
    key_weight = noise(seeds[4], (KVH * HD, D), D ** -0.5, 0.125, ((0, 2),))
    value_weight = noise(seeds[5], (KVH * HD, D), D ** -0.5, 0.125, ((0, 2),))
    headgate_weight = noise(seeds[6], (H, D), D ** -0.5, 0.125, ((0, 2),))
    merge_weight = noise(seeds[7], (D, H * HD), (D // 64) ** -0.5, 1.0, ((1, 2),))
    query_norm = jnp.clip(jax.random.uniform(seeds[8], (HD,), jnp.float32, 0.8984375, 2.0), 0.8984375, 2.0).astype(jnp.bfloat16)
    key_norm = jnp.clip(jax.random.uniform(seeds[9], (HD,), jnp.float32, 0.8984375, 2.0), 0.8984375, 2.0).astype(jnp.bfloat16)
    second_gain = jnp.clip(1.0 + 0.15 * jax.random.normal(seeds[10], (D,), jnp.float32), 0.25, 1.75).astype(jnp.bfloat16)
    gate_weight = noise(seeds[11], (FF, D), D ** -0.5, 0.125, ((0, 32),))
    up_weight = noise(seeds[12], (FF, D), D ** -0.5, 0.125, ((0, 32),))
    down_weight = noise(seeds[13], (FF, D), FF ** -0.5, 0.078125, ((0, 32),))
    out_cotangent = draw_out_cotangent(jax.random.fold_in(seeds[15], 71), 0)
    return dict(tokens=tokens, item_lengths=item_lengths, first_gain=first_gain, query_weight=query_weight, key_weight=key_weight, value_weight=value_weight, headgate_weight=headgate_weight, merge_weight=merge_weight, query_norm=query_norm, key_norm=key_norm, second_gain=second_gain, gate_weight=gate_weight, up_weight=up_weight, down_weight=down_weight, out_cotangent=out_cotangent)


EPS = 1e-06
THETA = 1000000.0
NEG = -1e+30
HIGH = lax.Precision.HIGHEST

@jax.custom_vjp
def low(v):
    return lax.optimization_barrier(v.astype(jnp.bfloat16)).astype(jnp.float32)

@jax.custom_vjp
def low_back(v):
    return v

def low_keep(v):
    return (low(v), None)

def low_pass(kept, grad):
    return (grad,)

def back_keep(v):
    return (v, None)

def back_low(kept, grad):
    return (low(grad),)
low.defvjp(low_keep, low_pass)
low_back.defvjp(back_keep, back_low)

def across(first_matrix, second_matrix):
    return lax.dot_general(first_matrix, second_matrix, (((1,), (1,)), ((), ())), precision=HIGH, preferred_element_type=jnp.float32)

def normalize(values, gain_vector):
    inverse = lax.rsqrt(lax.optimization_barrier(jnp.mean(values * values, axis=-1, keepdims=True)) + EPS)
    return values * inverse * gain_vector

def rotary_tables(positions, head_width):
    half_width = head_width // 2
    frequency = THETA ** (-2.0 * jnp.arange(half_width, dtype=jnp.float32) / head_width)
    angles = positions.astype(jnp.float32)[:, None] * frequency[None, :]
    return (jnp.cos(angles)[:, None, :], jnp.sin(angles)[:, None, :])

def rotate(values, cosine_table, sine_table):
    half_width = values.shape[-1] // 2
    former = values[..., :half_width]
    latter = values[..., half_width:]
    return jnp.concatenate([former * cosine_table - latter * sine_table, latter * cosine_table + former * sine_table], axis=-1)

def item_geometry(item_lengths, first_row, row_count):
    item_ends = jnp.cumsum(item_lengths).astype(jnp.int32)
    item_starts = (item_ends - item_lengths).astype(jnp.int32)
    row_index = (first_row + jnp.arange(row_count, dtype=jnp.int32)).astype(jnp.int32)
    begins = lax.optimization_barrier(jnp.max(jnp.where(item_starts[None, :] <= row_index[:, None], item_starts[None, :], 0), axis=1)).astype(jnp.int32)
    return (row_index, begins)

def attend_block(inputs, all_keys, all_values, score_scale):
    queries, row_index, begins = inputs
    scores = jnp.einsum('rkgd,skd->kgrs', queries, all_keys, precision=HIGH) * score_scale
    scores = low_back(scores)
    key_index = jnp.arange(all_keys.shape[0], dtype=jnp.int32)
    valid = (key_index[None, :] >= begins[:, None]) & (key_index[None, :] <= row_index[:, None])
    scores = jnp.where(valid, scores, NEG)
    highest = lax.optimization_barrier(jnp.max(scores, axis=-1, keepdims=True))
    expo = jnp.where(valid, jnp.exp(scores - highest), 0.0)
    probs = low(expo / lax.optimization_barrier(jnp.sum(expo, axis=-1, keepdims=True)))
    return jnp.einsum('kgrs,skd->rkgd', probs, all_values, precision=HIGH)

def layer(params, item_lengths):
    residual, first_gain, query_weight, key_weight, value_weight, headgate_weight, merge_weight, query_norm, key_norm, second_gain, gate_weight, up_weight, down_weight = params
    total_rows = residual.shape[0]
    head_width = query_norm.shape[0]
    head_count = query_weight.shape[0] // head_width
    group_count = key_weight.shape[0] // head_width
    group_size = head_count // group_count
    row_index, begins = item_geometry(item_lengths, 0, total_rows)
    cosine_table, sine_table = rotary_tables(row_index - begins, head_width)
    normed = low(normalize(residual, first_gain))
    query_raw = low_back(across(normed, query_weight)).reshape(total_rows, head_count, head_width)
    key_raw = low_back(across(normed, key_weight)).reshape(total_rows, group_count, head_width)
    value_heads = low(low_back(across(normed, value_weight))).reshape(total_rows, group_count, head_width)
    gate_logit = low_back(across(normed, headgate_weight))
    queries = low(rotate(normalize(query_raw, query_norm), cosine_table, sine_table))
    all_keys = low(rotate(normalize(key_raw, key_norm), cosine_table, sine_table))
    block_rows = math.gcd(total_rows, 512)
    block_count = total_rows // block_rows
    grouped = queries.reshape(block_count, block_rows, group_count, group_size, head_width)
    attend = jax.checkpoint(partial(attend_block, all_keys=all_keys, all_values=value_heads, score_scale=1.0 / math.sqrt(head_width)))
    attended = lax.map(attend, (grouped, row_index.reshape(block_count, block_rows), begins.reshape(block_count, block_rows)))
    attended = low_back(attended.reshape(total_rows, head_count, head_width))
    gated = low((attended * jax.nn.sigmoid(gate_logit)[..., None]).reshape(total_rows, head_count * head_width))
    hidden = residual + low_back(across(gated, merge_weight))
    normed_second = low(normalize(hidden, second_gain))
    gate_pre = low_back(across(normed_second, gate_weight))
    up_pre = low_back(across(normed_second, up_weight))
    activation = low(jax.nn.silu(gate_pre) * up_pre)
    return hidden + low_back(jnp.dot(activation, down_weight, precision=HIGH, preferred_element_type=jnp.float32))

def reference(tokens, item_lengths, first_gain, query_weight, key_weight, value_weight, headgate_weight, merge_weight, query_norm, key_norm, second_gain, gate_weight, up_weight, down_weight, out_cotangent):
    params = tuple((array.astype(jnp.float32) for array in (tokens, first_gain, query_weight, key_weight, value_weight, headgate_weight, merge_weight, query_norm, key_norm, second_gain, gate_weight, up_weight, down_weight)))

    def wrapped(*inputs):
        return layer(inputs, item_lengths)
    output, pullback = jax.vjp(wrapped, *params)
    grads = pullback(out_cotangent.astype(jnp.float32))
    return (output.astype(jnp.bfloat16), grads[0], grads[1], grads[2], grads[3], grads[4], grads[5], grads[6], grads[7], grads[8], grads[9], grads[10], grads[11], grads[12])
```

```python
import math

import jax
import jax.numpy as jnp
from jax import lax
from jax.sharding import PartitionSpec as P

EPS = 1e-06
THETA = 1000000.0
NEG = -1e30
F32 = jnp.float32
BF16 = jnp.bfloat16


def right_dot(first_matrix, second_matrix, kind=F32):
    return lax.dot_general(
        first_matrix, second_matrix, (((1,), (1,)), ((), ())), preferred_element_type=F32
    ).astype(kind)


def plain_dot(first_matrix, second_matrix, kind=F32):
    return jnp.dot(first_matrix, second_matrix, preferred_element_type=F32).astype(kind)


def outer_dot(first_matrix, second_matrix, kind=F32):
    return lax.dot_general(
        first_matrix, second_matrix, (((0,), (0,)), ((), ())), preferred_element_type=F32
    ).astype(kind)


def normalize(values, gain_vector):
    inverse = lax.rsqrt(jnp.mean(values * values, axis=-1, keepdims=True) + EPS)
    return (values * inverse * gain_vector, inverse)


def normalize_back(values, inverse, gain_vector, upstream):
    weighted = upstream * gain_vector
    inner_mean = jnp.mean(weighted * values, axis=-1, keepdims=True)
    return (
        inverse * weighted - values * inverse * inverse * inverse * inner_mean,
        values * inverse * upstream,
    )


def rotary_tables(positions, head_width):
    half_width = head_width // 2
    frequency = THETA ** (-2.0 * jnp.arange(half_width, dtype=F32) / head_width)
    angles = positions.astype(F32)[:, None] * frequency[None, :]
    return (jnp.cos(angles)[:, None, :], jnp.sin(angles)[:, None, :])


def rotate(values, cosine_table, sine_table):
    half_width = values.shape[-1] // 2
    former = values[..., :half_width]
    latter = values[..., half_width:]
    return jnp.concatenate(
        [former * cosine_table - latter * sine_table, latter * cosine_table + former * sine_table],
        axis=-1,
    )


def swiglu_back(gate_pre, up_pre, grad_act):
    sigma = jax.nn.sigmoid(gate_pre)
    grad_gate = grad_act * up_pre * sigma * (1.0 + gate_pre * (1.0 - sigma))
    grad_up = grad_act * gate_pre * sigma
    return (grad_gate.astype(BF16), grad_up.astype(BF16))


def exchange(values, mask):
    size = lax.axis_size("sp")
    return lax.ppermute(values, "sp", [(i, i ^ mask) for i in range(size)])


def swap(values):
    return lax.ppermute(values, "tp", [(0, 1), (1, 0)])


def stack_rows(*pieces):
    return jnp.concatenate(pieces, axis=0)


def stack_columns(*pieces):
    return jnp.concatenate(pieces, axis=1)


def gather_over(values, masks):
    for mask in masks:
        values = stack_rows(values, exchange(values, mask))
    return values


def gather_direct(values, masks):
    return stack_rows(values, *[exchange(values, mask) for mask in masks])


def scatter_over(values, masks):
    for mask in reversed(masks):
        kept = values.shape[0] // 2
        arrived = exchange(values[kept:].astype(BF16), mask)
        values = values[:kept].astype(F32) + arrived.astype(F32)
    return values


def scatter_direct(values, masks):
    rows = values.shape[0] // (len(masks) + 1)
    total = values[:rows].astype(F32)
    for place, mask in enumerate(masks, start=1):
        piece = values[place * rows : (place + 1) * rows].astype(BF16)
        total = total + exchange(piece, mask).astype(F32)
    return total


def rows_at(values, start, count):
    return lax.dynamic_slice_in_dim(values, start, count, axis=0)


def columns_at(values, start, count):
    return lax.dynamic_slice_in_dim(values, start, count, axis=1)


def shards(
    tokens,
    item_lengths,
    first_gain,
    query_weight,
    key_weight,
    value_weight,
    headgate_weight,
    merge_weight,
    query_norm,
    key_norm,
    second_gain,
    gate_weight,
    up_weight,
    down_weight,
    out_cotangent,
):
    sp_size = lax.axis_size("sp")
    device = lax.axis_index("sp")
    side = lax.axis_index("tp")
    local_rows, width = tokens.shape
    half_rows = local_rows // 2
    head_width = query_norm.shape[0]
    local_heads = query_weight.shape[0] // head_width
    groups = key_weight.shape[0] // head_width
    group_size = local_heads // groups
    query_width = group_size * head_width
    score_scale = 1.0 / math.sqrt(head_width)

    bits = sp_size.bit_length() - 1
    group_step = 1 << (bits // 2)
    group_masks = [group_step * k for k in range(1, groups)]
    all_group_masks = [0] + group_masks
    group_bits = group_step * (groups - 1)
    rest = [1 << b for b in range(1, bits) if not (1 << b) & group_bits] + [1]
    rest_count = 1 << len(rest)
    rest_masks = [
        sum(mask for b, mask in enumerate(rest) if r >> b & 1) for r in range(rest_count)
    ]
    own_group = (device // group_step) % groups
    own_rest = sum(((device // mask) % 2) * (1 << b) for b, mask in enumerate(rest))

    residual = tokens.astype(F32)
    first_gain_f = first_gain.astype(F32)
    second_gain_f = second_gain.astype(F32)
    query_gain = query_norm.astype(F32)
    key_gain = key_norm.astype(F32)

    normed, first_inverse = normalize(residual, first_gain_f)
    normed_low = normed.astype(BF16)
    query_own = right_dot(normed_low, query_weight, BF16)
    key_own = right_dot(normed_low, key_weight, BF16)
    value_own = right_dot(normed_low, value_weight, BF16)
    gate_value = jax.nn.sigmoid(right_dot(normed_low, headgate_weight))

    def group_columns(values, group, count):
        return columns_at(values, group * count, count)

    arrived = []
    for mask_place, mask in enumerate(all_group_masks):
        group = own_group ^ mask_place
        piece = stack_columns(
            group_columns(query_own, group, query_width),
            group_columns(key_own, group, head_width),
            group_columns(value_own, group, head_width),
        )
        arrived.append(exchange(piece, mask) if mask else piece)
    head_rows = stack_rows(*arrived)
    owned = head_rows.shape[0]

    item_ends = jnp.cumsum(item_lengths)
    item_starts = item_ends - item_lengths

    def begins_of(row_index):
        return jnp.max(
            jnp.where(item_starts[None, :] <= row_index[:, None], item_starts[None, :], 0), axis=1
        )

    within = jnp.arange(local_rows, dtype=jnp.int32)

    def rows_from(mask):
        return (device ^ mask) * local_rows + within

    row_index = jnp.concatenate([rows_from(mask) for mask in all_group_masks])
    key_index = jnp.concatenate(
        [rows_from(outer ^ mask) for outer in rest_masks for mask in all_group_masks]
    )
    begins = begins_of(row_index)
    cosine_table, sine_table = rotary_tables(row_index - begins, head_width)

    query_raw = head_rows[:, :query_width].astype(F32).reshape(owned, group_size, head_width)
    key_raw = head_rows[:, query_width : query_width + head_width].astype(F32)
    key_raw = key_raw.reshape(owned, 1, head_width)
    query_unit, query_inverse = normalize(query_raw, query_gain)
    key_unit, key_inverse = normalize(key_raw, key_gain)
    queries = rotate(query_unit, cosine_table, sine_table).astype(BF16)
    keys_low = rotate(key_unit, cosine_table, sine_table).astype(BF16)[:, 0]
    pair_all = gather_over(stack_columns(keys_low, head_rows[:, query_width + head_width :]), rest)
    keys_all, values_all = pair_all[:, :head_width], pair_all[:, head_width:]

    valid = (key_index[None, :] >= begins[:, None]) & (key_index[None, :] <= row_index[:, None])
    scores = jnp.einsum("rgd,sd->grs", queries, keys_all, preferred_element_type=F32) * score_scale
    scores = jnp.where(valid, scores, NEG)
    highest = jnp.max(scores, axis=-1, keepdims=True)
    expo = jnp.where(valid, jnp.exp(scores - highest), 0.0)
    probs = expo / jnp.sum(expo, axis=-1, keepdims=True)
    probs_low = probs.astype(BF16)
    attended = jnp.einsum("grs,sd->rgd", probs_low, values_all, preferred_element_type=F32)

    def to_row_owner(values):
        pieces = [
            exchange(values[k * local_rows : (k + 1) * local_rows], mask)
            if mask
            else values[:local_rows]
            for k, mask in enumerate(all_group_masks)
        ]
        stacked = jnp.stack(pieces)
        return [
            lax.dynamic_index_in_dim(stacked, own_group ^ g, axis=0, keepdims=False)
            for g in range(groups)
        ]

    attended_low = attended.reshape(owned, query_width).astype(BF16)
    attended_rows = stack_columns(*to_row_owner(attended_low)).astype(F32)
    attended_rows = attended_rows.reshape(local_rows, local_heads, head_width)
    gated_low = (attended_rows * gate_value[..., None]).astype(BF16).reshape(local_rows, -1)
    attention_part = right_dot(gated_low, merge_weight)
    arrived_part = swap(rows_at(attention_part, (1 - side) * half_rows, half_rows).astype(BF16))
    attention_out = rows_at(attention_part, side * half_rows, half_rows) + arrived_part.astype(F32)
    hidden = rows_at(residual, side * half_rows, half_rows) + attention_out
    normed_second, second_inverse = normalize(hidden, second_gain_f)
    second_low = normed_second.astype(BF16)

    def units(weight):
        both = stack_rows(weight, swap(weight))
        return stack_rows(both, exchange(both, 1))

    gate_units, up_units, down_units = units(gate_weight), units(up_weight), units(down_weight)
    row_masks = rest[:-1]
    grad_half = rows_at(out_cotangent, side * half_rows, half_rows)
    grads_low = gather_over(gather_direct(grad_half, group_masks), row_masks)
    inputs_low = gather_over(gather_direct(second_low, group_masks), row_masks)
    gate_pre = right_dot(inputs_low, gate_units)
    up_pre = right_dot(inputs_low, up_units)
    act_low = (jax.nn.silu(gate_pre) * up_pre).astype(BF16)
    grad_act = right_dot(grads_low, down_units)
    grad_gate, grad_up = swiglu_back(gate_pre, up_pre, grad_act)

    def to_rows(values):
        return scatter_direct(scatter_over(values, row_masks), group_masks)

    grad_second = to_rows(plain_dot(grad_gate, gate_units) + plain_dot(grad_up, up_units))
    branch_out = to_rows(plain_dot(act_low, down_units))

    def own_units(first_matrix, second_matrix):
        values = outer_dot(first_matrix, second_matrix)
        kept = values.shape[0] // 2
        values = values[:kept] + exchange(values[kept:].astype(BF16), 1).astype(F32)
        kept = kept // 2
        return values[:kept] + swap(values[kept:].astype(BF16)).astype(F32)

    gate_acc = own_units(grad_gate, inputs_low)
    up_acc = own_units(grad_up, inputs_low)
    down_acc = own_units(act_low, grads_low)

    def both_sides(values):
        other = swap(values)
        return jnp.where(side == 0, stack_rows(values, other), stack_rows(other, values))

    layer_output = both_sides((hidden + branch_out).astype(BF16))
    grad_hidden_norm, second_terms = normalize_back(
        hidden, second_inverse, second_gain_f, grad_second
    )
    hidden_low = both_sides((grad_half.astype(F32) + grad_hidden_norm).astype(BF16))

    grad_gated = plain_dot(hidden_low, merge_weight).reshape(local_rows, local_heads, head_width)
    grad_attended_low = (grad_gated * gate_value[..., None]).astype(BF16).reshape(local_rows, -1)
    grad_logit_low = (
        jnp.sum(grad_gated * attended_rows, axis=-1) * gate_value * (1.0 - gate_value)
    ).astype(BF16)
    arrived = []
    for mask_place, mask in enumerate(all_group_masks):
        piece = group_columns(grad_attended_low, own_group ^ mask_place, query_width)
        arrived.append(exchange(piece, mask) if mask else piece)
    grad_grouped = stack_rows(*arrived).reshape(owned, group_size, head_width)
    row_delta = jnp.sum(grad_grouped.astype(F32) * attended, axis=-1).T
    grad_probs = jnp.einsum("rgd,sd->grs", grad_grouped, values_all, preferred_element_type=F32)
    grad_scores = (probs * (grad_probs - row_delta[..., None])).astype(BF16)
    grad_queries = (
        jnp.einsum("grs,sd->rgd", grad_scores, keys_all, preferred_element_type=F32) * score_scale
    )
    grad_keys = (
        jnp.einsum("grs,rgd->sd", grad_scores, queries, preferred_element_type=F32) * score_scale
    )
    grad_values = jnp.einsum("grs,rgd->sd", probs_low, grad_grouped, preferred_element_type=F32)
    pair_sum = scatter_over(stack_columns(grad_keys, grad_values), rest)

    grad_query_raw, query_gain_terms = normalize_back(
        query_raw, query_inverse, query_gain, rotate(grad_queries, cosine_table, -sine_table)
    )
    grad_key_unit = pair_sum[:, :head_width].reshape(owned, 1, head_width)
    grad_key_raw, key_gain_terms = normalize_back(
        key_raw, key_inverse, key_gain, rotate(grad_key_unit, cosine_table, -sine_table)
    )
    grad_head_rows = stack_columns(
        grad_query_raw.reshape(owned, query_width).astype(BF16),
        grad_key_raw.reshape(owned, head_width).astype(BF16),
        pair_sum[:, head_width:].astype(BF16),
    )

    back = to_row_owner(grad_head_rows)
    query_low = stack_columns(*[b[:, :query_width] for b in back])
    key_low = stack_columns(*[b[:, query_width : query_width + head_width] for b in back])
    value_low = stack_columns(*[b[:, query_width + head_width :] for b in back])
    input_part = (
        plain_dot(query_low, query_weight)
        + plain_dot(key_low, key_weight)
        + plain_dot(value_low, value_weight)
        + plain_dot(grad_logit_low, headgate_weight)
    ).astype(BF16)
    input_sum = input_part.astype(F32) + swap(input_part).astype(F32)
    grad_residual_norm, first_terms = normalize_back(
        residual, first_inverse, first_gain_f, input_sum
    )
    input_grad = hidden_low.astype(F32) + grad_residual_norm

    block = width // rest_count
    normed_half = rows_at(normed_low, side * half_rows, half_rows)
    normed_half = stack_columns(
        *[columns_at(normed_half, (own_rest ^ r) * block, block) for r in range(rest_count)]
    )
    normed_side = gather_direct(normed_half, group_masks)
    normed_owned = stack_rows(normed_side, swap(normed_side))
    halves = grad_head_rows.reshape(groups, 2, half_rows, -1)
    halves = jnp.where(side == 0, halves, halves[:, ::-1])
    halves = jnp.transpose(halves, (1, 0, 2, 3)).reshape(owned, -1)
    head_grads = outer_dot(halves, normed_owned)
    for mask in reversed(rest):
        kept = head_grads.shape[1] // 2
        head_grads = head_grads[:, :kept] + exchange(
            head_grads[:, kept:].astype(BF16), mask
        ).astype(F32)
    head_blocks = gather_over(gather_direct(head_grads.astype(BF16), group_masks), rest)
    head_blocks = head_blocks.reshape(sp_size, -1, block)
    query_grad = jnp.zeros(query_weight.shape, F32)
    key_grad = jnp.zeros(key_weight.shape, F32)
    value_grad = jnp.zeros(value_weight.shape, F32)
    for r in range(rest_count):
        for k in range(groups):
            piece = head_blocks[r * groups + k].astype(F32)
            group, column = own_group ^ k, (own_rest ^ r) * block
            query_grad = lax.dynamic_update_slice(
                query_grad, piece[:query_width], (group * query_width, column)
            )
            key_grad = lax.dynamic_update_slice(
                key_grad, piece[query_width : query_width + head_width], (group * head_width, column)
            )
            value_grad = lax.dynamic_update_slice(
                value_grad, piece[query_width + head_width :], (group * head_width, column)
            )

    strip = width // sp_size
    order = [outer ^ mask for outer in rest_masks for mask in all_group_masks]
    hidden_relative = stack_columns(
        *[columns_at(hidden_low, (device ^ mask) * strip, strip) for mask in order]
    )
    merge_part = outer_dot(hidden_relative, gated_low)
    merge_part = scatter_direct(scatter_over(merge_part, rest), group_masks)
    merge_blocks = gather_over(gather_direct(merge_part.astype(BF16), group_masks), rest)
    merge_grad = jnp.zeros(merge_weight.shape, F32)
    for place, mask in enumerate(order):
        merge_grad = lax.dynamic_update_slice(
            merge_grad,
            merge_blocks[place * strip : (place + 1) * strip].astype(F32),
            ((device ^ mask) * strip, 0),
        )

    headgate_part = outer_dot(grad_logit_low, normed_low)
    gains = jnp.concatenate(
        [
            jnp.sum(query_gain_terms, axis=(0, 1)),
            jnp.sum(key_gain_terms, axis=(0, 1)),
            jnp.zeros((width - 2 * head_width,), F32),
        ]
    )
    sides = jnp.stack([jnp.sum(second_terms, axis=0), gains])
    sides = sides + swap(sides)
    small = stack_rows(headgate_part, jnp.sum(first_terms, axis=0)[None], sides)
    for b in range(bits):
        small = small + exchange(small, 1 << b)

    return (
        layer_output,
        input_grad,
        small[local_heads],
        query_grad,
        key_grad,
        value_grad,
        small[:local_heads],
        merge_grad,
        small[local_heads + 2, :head_width],
        small[local_heads + 2, head_width : 2 * head_width],
        small[local_heads + 1],
        gate_acc,
        up_acc,
        down_acc,
    )


def solution(mesh):
    return jax.shard_map(
        shards,
        mesh=mesh,
        in_specs=(
            P("sp", None),
            P(),
            P(),
            P("tp", None),
            P("tp", None),
            P("tp", None),
            P("tp", None),
            P(None, "tp"),
            P(),
            P(),
            P(),
            P(("tp", "sp"), None),
            P(("tp", "sp"), None),
            P(("tp", "sp"), None),
            P("sp", None),
        ),
        out_specs=(
            P("sp", None),
            P("sp", None),
            P(),
            P("tp", None),
            P("tp", None),
            P("tp", None),
            P("tp", None),
            P(None, "tp"),
            P(),
            P(),
            P(),
            P(("tp", "sp"), None),
            P(("tp", "sp"), None),
            P(("tp", "sp"), None),
        ),
        check_vma=False,
    )
```

```python
import math

import jax
import jax.numpy as jnp
from jax import lax
from jax.experimental import pallas as pl
from jax.experimental.pallas import tpu as pltpu
from jax.sharding import PartitionSpec as P

EPS = 1e-06
THETA = 1000000.0
NEG = -1e30
F32 = jnp.float32
BF16 = jnp.bfloat16


def right_dot(first_matrix, second_matrix, kind=F32):
    return lax.dot_general(
        first_matrix, second_matrix, (((1,), (1,)), ((), ())), preferred_element_type=F32
    ).astype(kind)


def plain_dot(first_matrix, second_matrix, kind=F32):
    return jnp.dot(first_matrix, second_matrix, preferred_element_type=F32).astype(kind)


def outer_dot(first_matrix, second_matrix, kind=F32):
    return lax.dot_general(
        first_matrix, second_matrix, (((0,), (0,)), ((), ())), preferred_element_type=F32
    ).astype(kind)


def normalize(values, gain_vector):
    inverse = lax.rsqrt(jnp.mean(values * values, axis=-1, keepdims=True) + EPS)
    return (values * inverse * gain_vector, inverse)


def normalize_back(values, inverse, gain_vector, upstream):
    weighted = upstream * gain_vector
    inner_mean = jnp.mean(weighted * values, axis=-1, keepdims=True)
    return (
        inverse * weighted - values * inverse * inverse * inverse * inner_mean,
        values * inverse * upstream,
    )


def rotary_tables(positions, head_width):
    half_width = head_width // 2
    frequency = THETA ** (-2.0 * jnp.arange(half_width, dtype=F32) / head_width)
    angles = positions.astype(F32)[:, None] * frequency[None, :]
    return (jnp.cos(angles)[:, None, :], jnp.sin(angles)[:, None, :])


def rotate(values, cosine_table, sine_table):
    half_width = values.shape[-1] // 2
    former = values[..., :half_width]
    latter = values[..., half_width:]
    return jnp.concatenate(
        [former * cosine_table - latter * sine_table, latter * cosine_table + former * sine_table],
        axis=-1,
    )


def swiglu_back(gate_pre, up_pre, grad_act):
    sigma = jax.nn.sigmoid(gate_pre)
    grad_gate = grad_act * up_pre * sigma * (1.0 + gate_pre * (1.0 - sigma))
    grad_up = grad_act * gate_pre * sigma
    return (grad_gate.astype(BF16), grad_up.astype(BF16))


def exchange(values, mask):
    size = lax.axis_size("sp")
    return lax.ppermute(values, "sp", [(i, i ^ mask) for i in range(size)])


def swap(values):
    return lax.ppermute(values, "tp", [(0, 1), (1, 0)])


def stack_rows(*pieces):
    return jnp.concatenate(pieces, axis=0)


def stack_columns(*pieces):
    return jnp.concatenate(pieces, axis=1)


def gather_over(values, masks):
    for mask in masks:
        values = stack_rows(values, exchange(values, mask))
    return values


def gather_direct(values, masks):
    return stack_rows(values, *[exchange(values, mask) for mask in masks])


def scatter_over(values, masks):
    for mask in reversed(masks):
        kept = values.shape[0] // 2
        arrived = exchange(values[kept:].astype(BF16), mask)
        values = values[:kept].astype(F32) + arrived.astype(F32)
    return values


def scatter_direct(values, masks):
    rows = values.shape[0] // (len(masks) + 1)
    total = values[:rows].astype(F32)
    for place, mask in enumerate(masks, start=1):
        piece = values[place * rows : (place + 1) * rows].astype(BF16)
        total = total + exchange(piece, mask).astype(F32)
    return total


def rows_at(values, start, count):
    return lax.dynamic_slice_in_dim(values, start, count, axis=0)


def columns_at(values, start, count):
    return lax.dynamic_slice_in_dim(values, start, count, axis=1)


def after_all(values, *others):
    return lax.optimization_barrier((tuple(values), others))[0]


def after(value, *others):
    return after_all((value,), *others)[0]


def whole(values):
    shape = values.shape
    return pl.BlockSpec(shape, lambda *_: (0,) * len(shape))


def call(body, outs, operands, in_specs=None, out_specs=None, grid=(1,), scalars=None, scratch=()):
    in_specs = [s or whole(v) for s, v in zip(in_specs or [None] * len(operands), operands)]
    out_specs = [s or whole(o) for s, o in zip(out_specs or [None] * len(outs), outs)]
    return pl.pallas_call(
        body,
        out_shape=outs,
        grid_spec=pltpu.PrefetchScalarGridSpec(
            num_scalar_prefetch=0 if scalars is None else 1,
            grid=grid,
            in_specs=in_specs,
            out_specs=out_specs,
            scratch_shapes=list(scratch),
        ),
        cost_estimate=pl.CostEstimate(flops=0, bytes_accessed=1024, transcendentals=0),
        compiler_params=pltpu.CompilerParams(vmem_limit_bytes=60 * 1024 * 1024),
    )(*([] if scalars is None else [scalars]), *operands)


def array(shape, kind):
    return jax.ShapeDtypeStruct(shape, kind)


def unit_rows(values):
    return values * lax.rsqrt(jnp.mean(values * values, axis=-1, keepdims=True) + EPS)


def project(tokens, gain, weights, headgate, cotangent, places, groups):
    rows, width = tokens.shape
    half = rows // 2
    sizes = [w.shape[0] // groups for w in weights]
    heads = headgate.shape[0]
    head_width = sizes[1]
    per_group = heads // groups
    middle = width // 2

    def body(at, x_ref, g_ref, q_ref, k_ref, v_ref, h_ref, c_ref, *refs):
        pieces, (normed_out, side_out, core_out, grad_out, gate_out, normed_s, gate_s) = (
            refs[:groups],
            refs[groups:],
        )
        step = pl.program_id(0)

        @pl.when(step == 0)
        def _():
            normed = (unit_rows(x_ref[...].astype(F32)) * g_ref[...].astype(F32)).astype(BF16)
            normed_s[...] = normed
            normed_out[...] = normed
            gate_s[...] = jax.nn.sigmoid(right_dot(normed, h_ref[...]))
            start = pl.multiple_of(at[groups] * half, half)
            grad_out[...] = c_ref[pl.ds(start, half), :]
            own = pl.multiple_of(at[groups + 1] * middle, middle)
            other = pl.multiple_of((1 - at[groups + 1]) * middle, middle)
            side_out[...] = normed_s[pl.ds(start, half), pl.ds(own, middle)]
            core_out[...] = normed_s[pl.ds(start, half), pl.ds(other, middle)]

        normed = normed_s[...]
        piece = jnp.concatenate(
            [right_dot(normed, w[...], BF16) for w in (q_ref, k_ref, v_ref)], axis=1
        )
        for place in range(groups):

            @pl.when(step == place)
            def _(place=place):
                pieces[place][...] = piece

        lane = lax.broadcasted_iota(jnp.int32, gate_s.shape, 1)
        for h in range(per_group):
            column = jnp.where(lane == at[step] * per_group + h, gate_s[...], 0.0)
            column = jnp.sum(column, axis=1, keepdims=True)
            gate_out[:, h * head_width : (h + 1) * head_width] = jnp.broadcast_to(
                column, (rows, head_width)
            )

    out = call(
        body,
        [array((rows, sum(sizes)), BF16)] * groups
        + [
            array((rows, width), BF16),
            array((half, middle), BF16),
            array((half, middle), BF16),
            array((half, width), BF16),
            array((groups * rows, per_group * head_width), F32),
        ],
        [tokens, gain, *weights, headgate, cotangent],
        [None, None]
        + [pl.BlockSpec((size, width), lambda k, at: (at[k], 0)) for size in sizes]
        + [None, None],
        [None] * (groups + 4)
        + [pl.BlockSpec((rows, per_group * head_width), lambda k, at: (k, 0))],
        grid=(groups,),
        scalars=places,
        scratch=[pltpu.VMEM((rows, width), BF16), pltpu.VMEM((rows, heads), F32)],
    )
    return (out[:groups], *out[groups:])


def turn(values, cosine, sine):
    return values * cosine + pltpu.roll(values, values.shape[-1] // 2, 1) * sine


def head_forward(pieces, cosine, sine, query_gain, key_gain):
    rows = pieces[0].shape[0]
    owned = rows * len(pieces)
    head_width = query_gain.shape[1]
    query_width = pieces[0].shape[1] - 2 * head_width

    def body(*refs):
        inputs = refs[: len(pieces)]
        cos_ref, sin_ref, qg_ref, kg_ref, q_out, kv_out = refs[len(pieces) :]
        for place, ref in enumerate(inputs):
            at = slice(place * rows, (place + 1) * rows)
            cos, sin = cos_ref[at, :], sin_ref[at, :]
            for first in range(0, query_width + head_width, head_width):
                gain = (qg_ref if first < query_width else kg_ref)[...]
                unit = unit_rows(ref[:, first : first + head_width].astype(F32)) * gain
                turned = turn(unit, cos, sin).astype(BF16)
                if first < query_width:
                    q_out[at, first : first + head_width] = turned
                else:
                    kv_out[at, :head_width] = turned
            kv_out[at, head_width:] = ref[:, query_width + head_width :]

    return call(
        body,
        [array((owned, query_width), BF16), array((owned, 2 * head_width), BF16)],
        [*pieces, cosine, sine, query_gain, key_gain],
    )


def head_backward(pieces, cosine, sine, query_gain, key_gain, grad_queries, pair_kept, pair_arrived):
    rows = pieces[0].shape[0]
    count = len(pieces)
    head_width = query_gain.shape[1]
    query_width = pieces[0].shape[1] - 2 * head_width

    def body(*refs):
        inputs = refs[:count]
        cos_ref, sin_ref, qg_ref, kg_ref, dq_ref, kept_ref, arrived_ref = refs[count : count + 7]
        outs, (stack_out, gains_out) = refs[count + 7 : 2 * count + 7], refs[2 * count + 7 :]
        gains = [jnp.zeros((1, head_width), F32) for _ in range(2)]
        for place, ref in enumerate(inputs):
            at = slice(place * rows, (place + 1) * rows)
            cos, sin = cos_ref[at, :], sin_ref[at, :]
            pair = kept_ref[at, :] + arrived_ref[at, :].astype(F32)
            for first in range(0, query_width + head_width, head_width):
                is_query = first < query_width
                gain = (qg_ref if is_query else kg_ref)[...]
                raw = ref[:, first : first + head_width].astype(F32)
                grad = dq_ref[at, first : first + head_width] if is_query else pair[:, :head_width]
                inverse = lax.rsqrt(jnp.mean(raw * raw, axis=-1, keepdims=True) + EPS)
                back, terms = normalize_back(raw, inverse, gain, turn(grad, cos, -sin))
                outs[place][:, first : first + head_width] = back.astype(BF16)
                which = 0 if is_query else 1
                gains[which] = gains[which] + jnp.sum(terms, axis=0, keepdims=True)
            outs[place][:, query_width + head_width :] = pair[:, head_width:].astype(BF16)
            stack_out[at, :] = outs[place][...]
        gains_out[0:1, :] = gains[0]
        gains_out[1:2, :] = gains[1]

    out = call(
        body,
        [array(pieces[0].shape, BF16)] * count
        + [array((count * rows, pieces[0].shape[1]), BF16), array((2, head_width), F32)],
        [*pieces, cosine, sine, query_gain, key_gain, grad_queries, pair_kept, pair_arrived],
    )
    return (out[:count], out[count], out[count + 1])


def stacked_heads(values, head_width):
    return jnp.concatenate(
        [values[:, h : h + head_width] for h in range(0, values.shape[1], head_width)], axis=0
    )


def unstacked_heads(values, rows):
    return jnp.concatenate(
        [values[h : h + rows] for h in range(0, values.shape[0], rows)], axis=1
    )


def key_chunk(total):
    return math.gcd(total, 512)


def chunk_loop(total, step):
    chunk = key_chunk(total)
    count = total // chunk
    if count <= 4:
        for index in range(count):
            step(index * chunk, chunk)
    else:
        pl.loop(0, count)(lambda index: step(pl.multiple_of(index * chunk, chunk), chunk))


def row_bounds(at, step, rows, items, blocks):
    row = at[items + step] + lax.broadcasted_iota(jnp.int32, (rows, 1), 0)
    begin = jnp.zeros((rows, 1), jnp.int32)
    for item in range(items):
        begin = jnp.maximum(begin, jnp.where(row >= at[item], at[item], 0))
    return (row, begin)


def masked_bias(key_ref, row, begin, start, chunk, copies):
    keys = key_ref[:, pl.ds(start, chunk)]
    bias = jnp.where((keys >= begin) & (keys <= row), 0.0, NEG)
    return jnp.concatenate([bias] * copies, axis=0)


def load_pairs(pairs, keys_s, values_s, head_width):
    start = 0
    for ref in pairs:
        rows = ref.shape[0]
        keys_s[start : start + rows, :] = ref[:, :head_width]
        values_s[start : start + rows, :] = ref[:, head_width:]
        start += rows


def attend(queries, pairs, key_index, bounds, blocks, score_scale):
    owned, query_width = queries.shape
    rows = owned // blocks
    head_width = pairs[0].shape[1] // 2
    copies = query_width // head_width
    total = key_index.shape[1]
    count = len(pairs)
    tall = rows * copies

    def body(at_rows, q_ref, *refs):
        pair_refs = refs[:count]
        key_ref, o_out, l_out = refs[count : count + 3]
        lows = refs[count + 3 : count + 3 + blocks]
        keys_s, values_s, scores_s, most_s, sum_s, acc_s = refs[count + 3 + blocks :]
        step = pl.program_id(0)
        row, begin = row_bounds(at_rows, step, rows, bounds.shape[0] - blocks, blocks)

        @pl.when(step == 0)
        def _():
            load_pairs(pair_refs, keys_s, values_s, head_width)

        query = stacked_heads(q_ref[...], head_width)
        most_s[...] = jnp.full(most_s.shape, NEG, F32)
        sum_s[...] = jnp.zeros(sum_s.shape, F32)
        acc_s[...] = jnp.zeros(acc_s.shape, F32)

        def first(start, chunk):
            at = pl.ds(start, chunk)
            scores = right_dot(query, keys_s[at, :]) * score_scale
            scores = scores + masked_bias(key_ref, row, begin, start, chunk, copies)
            scores_s[:, at] = scores
            most_s[...] = jnp.maximum(most_s[...], jnp.max(scores, axis=1, keepdims=True))

        def second(start, chunk):
            at = pl.ds(start, chunk)
            expo = jnp.exp(scores_s[:, at] - most_s[...])
            scores_s[:, at] = expo
            sum_s[...] += jnp.sum(expo, axis=1, keepdims=True)

        chunk_loop(total, first)
        chunk_loop(total, second)
        inverse = 1.0 / sum_s[...]

        def third(start, chunk):
            at = pl.ds(start, chunk)
            probs = (scores_s[:, at] * inverse).astype(BF16)
            acc_s[...] += plain_dot(probs, values_s[at, :])

        chunk_loop(total, third)
        attended = unstacked_heads(acc_s[...], rows)
        o_out[...] = attended
        log_sum = jnp.broadcast_to(most_s[...] + jnp.log(sum_s[...]), (tall, head_width))
        l_out[...] = unstacked_heads(log_sum, rows)
        for place in range(blocks):

            @pl.when(step == place)
            def _(place=place):
                lows[place][...] = attended.astype(BF16)

    def by_step(shape):
        return pl.BlockSpec(shape, lambda i, at: (i, 0))

    out = call(
        body,
        [array((owned, query_width), F32)] * 2 + [array((rows, query_width), BF16)] * blocks,
        [queries, *pairs, key_index],
        [by_step((rows, query_width))] + [None] * (count + 1),
        [by_step((rows, query_width))] * 2 + [None] * blocks,
        grid=(blocks,),
        scalars=bounds,
        scratch=[
            pltpu.VMEM((total, head_width), BF16),
            pltpu.VMEM((total, head_width), BF16),
            pltpu.VMEM((tall, total), F32),
            pltpu.VMEM((tall, 1), F32),
            pltpu.VMEM((tall, 1), F32),
            pltpu.VMEM((tall, head_width), F32),
        ],
    )
    return (out[0], out[1], out[2:])


def attend_back(queries, pairs, key_index, bounds, grads, attended, log_sums, score_scale):
    blocks = len(grads)
    owned, query_width = queries.shape
    rows = owned // blocks
    head_width = pairs[0].shape[1] // 2
    copies = query_width // head_width
    total = key_index.shape[1]
    count = len(pairs)
    tall = rows * copies
    half = total // 2

    def body(at_rows, q_ref, o_ref, l_ref, *refs):
        pair_refs, grad_refs = refs[:count], refs[count : count + blocks]
        key_ref, dq_out, kept_out, sent_out = refs[count + blocks : count + blocks + 4]
        keys_s, values_s, grads_s, dq_s, pair_s = refs[count + blocks + 4 :]
        step = pl.program_id(0)
        row, begin = row_bounds(at_rows, step, rows, bounds.shape[0] - blocks, blocks)

        @pl.when(step == 0)
        def _():
            load_pairs(pair_refs, keys_s, values_s, head_width)
            for place, ref in enumerate(grad_refs):
                grads_s[place] = ref[...]
            pair_s[...] = jnp.zeros(pair_s.shape, F32)

        query = stacked_heads(q_ref[...], head_width)
        grad = stacked_heads(grads_s[step], head_width)
        out = stacked_heads(o_ref[...], head_width)
        log_sum = stacked_heads(l_ref[...], head_width)[:, :1]
        delta = jnp.sum(grad.astype(F32) * out, axis=1, keepdims=True)
        dq_s[...] = jnp.zeros(dq_s.shape, F32)

        def each(start, chunk):
            at = pl.ds(start, chunk)
            keys, values = keys_s[at, :], values_s[at, :]
            scores = right_dot(query, keys) * score_scale
            scores = scores + masked_bias(key_ref, row, begin, start, chunk, copies)
            probs = jnp.exp(scores - log_sum)
            grad_scores = (probs * (right_dot(grad, values) - delta)).astype(BF16)
            dq_s[...] += plain_dot(grad_scores, keys)
            pair_s[at, :head_width] += outer_dot(grad_scores, query) * score_scale
            pair_s[at, head_width:] += outer_dot(probs.astype(BF16), grad)

        chunk_loop(total, each)
        dq_out[...] = unstacked_heads(dq_s[...], rows) * score_scale

        @pl.when(step == blocks - 1)
        def _():
            kept_out[...] = pair_s[:half, :]
            sent_out[...] = pair_s[half:, :].astype(BF16)

    def by_step(shape):
        return pl.BlockSpec(shape, lambda i, at: (i, 0))

    return call(
        body,
        [
            array((owned, query_width), F32),
            array((half, 2 * head_width), F32),
            array((half, 2 * head_width), BF16),
        ],
        [queries, attended, log_sums, *pairs, *grads, key_index],
        [by_step((rows, query_width))] * 3 + [None] * (count + blocks + 1),
        [by_step((rows, query_width)), None, None],
        grid=(blocks,),
        scalars=bounds,
        scratch=[
            pltpu.VMEM((total, head_width), BF16),
            pltpu.VMEM((total, head_width), BF16),
            pltpu.VMEM((blocks, rows, query_width), BF16),
            pltpu.VMEM((tall, head_width), F32),
            pltpu.VMEM((total, 2 * head_width), F32),
        ],
    )


def merge(attended, gate_value, merge_weight, tokens, places):
    groups = len(attended)
    rows, query_width = attended[0].shape
    width = tokens.shape[1]
    half = rows // 2

    def body(at, g_ref, w_ref, x_ref, *refs):
        inputs = refs[:groups]
        gated_out, sent_out, kept_out, stack_s, acc_s = refs[groups:]
        step = pl.program_id(0)

        @pl.when(step == 0)
        def _():
            for place, ref in enumerate(inputs):
                stack_s[place] = ref[...]
            acc_s[...] = jnp.zeros(acc_s.shape, F32)

        gated = (stack_s[step].astype(F32) * g_ref[...]).astype(BF16)
        gated_out[...] = gated
        acc_s[...] += right_dot(gated, w_ref[...])

        @pl.when(step == groups - 1)
        def _():
            own = pl.multiple_of(at[groups] * half, half)
            other = pl.multiple_of((1 - at[groups]) * half, half)
            sent_out[...] = acc_s[pl.ds(other, half), :].astype(BF16)
            kept_out[...] = acc_s[pl.ds(own, half), :] + x_ref[pl.ds(own, half), :].astype(F32)

    return call(
        body,
        [
            array((rows, groups * query_width), BF16),
            array((half, width), BF16),
            array((half, width), F32),
        ],
        [gate_value, merge_weight, tokens, *attended],
        [
            pl.BlockSpec((rows, query_width), lambda k, at: (k, 0)),
            pl.BlockSpec((width, query_width), lambda k, at: (0, at[k])),
            None,
        ]
        + [None] * groups,
        [pl.BlockSpec((rows, query_width), lambda k, at: (0, at[k])), None, None],
        grid=(groups,),
        scalars=places,
        scratch=[
            pltpu.VMEM((groups, rows, query_width), BF16),
            pltpu.VMEM((rows, width), F32),
        ],
    )


def second_norm(kept, arrived, gain):
    def body(kept_ref, arrived_ref, gain_ref, hidden_out, normed_out):
        hidden = kept_ref[...] + arrived_ref[...].astype(F32)
        hidden_out[...] = hidden
        normed_out[...] = (unit_rows(hidden) * gain_ref[...].astype(F32)).astype(BF16)

    return call(body, [array(kept.shape, F32), array(kept.shape, BF16)], [kept, arrived, gain])


def unit_copies(sources, which, target, semaphores):
    count = sources[0].shape[0] // 3
    return [
        pltpu.make_async_copy(
            source.at[pl.ds(which * count, count), :],
            target.at[pl.ds(place * count, count), :],
            semaphores.at[place],
        )
        for place, source in enumerate(sources)
    ]


def anywhere(values):
    return [pl.BlockSpec(memory_space=pl.ANY) for _ in values]


def fill_rows(pieces, target):
    start = 0
    for ref in pieces:
        target[start : start + ref.shape[0], :] = ref[...]
        start += ref.shape[0]


def act_gradient(pieces, stacks):
    rows, width = sum(piece.shape[0] for piece in pieces), pieces[0].shape[1]
    count, blocks = len(pieces), len(stacks)
    hidden = stacks[0].shape[0] // 3 * blocks
    half = hidden // 2

    def body(*refs):
        inputs, sources = refs[:count], refs[count : count + blocks]
        rows_out, grad_out, down_s, sems = refs[count + blocks :]
        copies = unit_copies(sources, 2, down_s, sems)
        for copy in copies:
            copy.start()
        fill_rows(inputs, rows_out)
        for h in range(2):
            for copy in copies[h * blocks // 2 : (h + 1) * blocks // 2]:
                copy.wait()
            grad_out[h] = right_dot(rows_out[...], down_s[h * half : (h + 1) * half, :])

    return call(
        body,
        [array((rows, width), BF16), array((2, rows, half), F32)],
        [*pieces, *stacks],
        [None] * count + anywhere(stacks),
        scratch=[pltpu.VMEM((hidden, width), BF16), pltpu.SemaphoreType.DMA((blocks,))],
    )


def feed(pieces, grad_act, stacks, part, kind):
    rows, width = sum(piece.shape[0] for piece in pieces), pieces[0].shape[1]
    count, blocks = len(pieces), len(stacks)
    hidden = stacks[0].shape[0] // 3 * blocks
    half = hidden // 2

    def body(*refs):
        inputs = refs[:count]
        grad_ref, sources = refs[count], refs[count + 1 : count + 1 + blocks]
        rows_out, left_out, sum_out, gate_s, up_s, sems = refs[count + 1 + blocks :]
        gate_copies = unit_copies(sources, 0, gate_s, sems.at[0])
        up_copies = unit_copies(sources, 1, up_s, sems.at[1])
        for pair in zip(gate_copies, up_copies):
            for copy in pair:
                copy.start()
        fill_rows(inputs, rows_out)
        for h in range(2):
            for place in range(h * blocks // 2, (h + 1) * blocks // 2):
                gate_copies[place].wait()
                up_copies[place].wait()
            at = slice(h * half, (h + 1) * half)
            gate_pre = right_dot(rows_out[...], gate_s[at, :])
            up_pre = right_dot(rows_out[...], up_s[at, :])
            sigma = jax.nn.sigmoid(gate_pre)
            grad = grad_ref[h]
            left_out[2, h] = (gate_pre * sigma * up_pre).astype(BF16)
            left_out[0, h] = (grad * up_pre * sigma * (1.0 + gate_pre * (1.0 - sigma))).astype(BF16)
            left_out[1, h] = (grad * gate_pre * sigma).astype(BF16)
        total = plain_dot(left_out[0, 0], gate_s[:half, :])
        total = total + plain_dot(left_out[0, 1], gate_s[half:, :])
        total = total + plain_dot(left_out[1, 0], up_s[:half, :])
        total = total + plain_dot(left_out[1, 1], up_s[half:, :])
        sum_out[...] = total.astype(kind)

    return call(
        body,
        [
            array((rows, width), BF16),
            array((3, 2, rows, half), BF16),
            array((rows, width), kind),
        ],
        [*pieces, grad_act, *stacks],
        [None] * count
        + [pl.BlockSpec((2, rows, half), lambda i: (0, part, 0))]
        + anywhere(stacks),
        scratch=[
            pltpu.VMEM((hidden, width), BF16),
            pltpu.VMEM((hidden, width), BF16),
            pltpu.SemaphoreType.DMA((2, blocks)),
        ],
    )


def branch(lefts, stacks):
    rows, half = lefts[0].shape[2:]
    width, blocks = stacks[0].shape[1], len(stacks)

    def body(near_ref, far_ref, *refs):
        kept_out, sent_out, down_s, sems = refs[blocks:]
        copies = unit_copies(refs[:blocks], 2, down_s, sems)
        for copy in copies:
            copy.start()
        for copy in copies:
            copy.wait()
        for act_ref, out in ((far_ref, sent_out), (near_ref, kept_out)):
            total = plain_dot(act_ref[0, 0], down_s[:half, :])
            total = total + plain_dot(act_ref[0, 1], down_s[half:, :])
            out[...] = total.astype(out.dtype)

    return call(
        body,
        [array((rows, width), F32), array((rows, width), BF16)],
        [*lefts, *stacks],
        [pl.BlockSpec((1, 2, rows, half), lambda i: (2, 0, 0, 0))] * 2 + anywhere(stacks),
        scratch=[pltpu.VMEM((2 * half, width), BF16), pltpu.SemaphoreType.DMA((blocks,))],
    )


def unit_gradients(lefts, inputs_low, grads_low):
    rows, half = lefts[0].shape[2:]
    width = grads_low.shape[1]

    def body(near_ref, far_ref, near_inputs, far_inputs, grads_ref, kept_out, sent_out):
        h, which = pl.program_id(0), pl.program_id(1)

        def put(near, far):
            value = outer_dot(near_ref[0, 0], near) + outer_dot(far_ref[0, 0], far)

            @pl.when(h == 0)
            def _():
                kept_out[...] = value

            @pl.when(h == 1)
            def _():
                sent_out[...] = value.astype(BF16)

        pl.when(which < 2)(lambda: put(near_inputs[...], far_inputs[...]))
        pl.when(which == 2)(lambda: put(grads_ref[:rows, :], grads_ref[rows:, :]))

    return call(
        body,
        [array((3 * half, width), F32), array((3 * half, width), BF16)],
        [*lefts, *inputs_low, grads_low],
        [pl.BlockSpec((1, 1, rows, half), lambda h, m: (m, h, 0, 0))] * 2 + [None] * 3,
        [
            pl.BlockSpec((half, width), lambda h, m: (jnp.where(h == 0, m, 2), 0)),
            pl.BlockSpec((half, width), lambda h, m: (jnp.where(h == 0, 0, m), 0)),
        ],
        grid=(2, 3),
    )


def add_units(kept, arrived):
    count, width = kept.shape[0] // 6, kept.shape[1]

    def body(kept_ref, arrived_ref, own_out, sent_out):
        own_out[...] = kept_ref[:count, :] + arrived_ref[:count, :].astype(F32)
        sent_out[...] = (kept_ref[count:, :] + arrived_ref[count:, :].astype(F32)).astype(BF16)

    return call(
        body,
        [array((3 * count, width), F32), array((3 * count, width), BF16)],
        [kept, arrived],
        [pl.BlockSpec((2 * count, width), lambda i: (i, 0))] * 2,
        [pl.BlockSpec((count, width), lambda i: (i, 0))] * 2,
        grid=(3,),
    )


def add_split(kept, arrived, parts):
    rows = kept.shape[0] // parts

    def body(kept_ref, arrived_ref, *outs):
        for place, out in enumerate(outs):
            at = slice(place * rows, (place + 1) * rows)
            out[...] = (kept_ref[at, :] + arrived_ref[at, :].astype(F32)).astype(out.dtype)

    shape = (rows, kept.shape[1])
    out = call(
        body, [array(shape, F32)] + [array(shape, BF16)] * (parts - 1), [kept, arrived]
    )
    return (out[0], out[1:])


def hidden_gradient(kept, arrived, hidden, gain, grad_half):
    rows, width = kept.shape

    def body(kept_ref, hidden_ref, gain_ref, grad_ref, *refs):
        low_out, terms_out = refs[-2:]
        upstream = kept_ref[...]
        for ref in refs[:-2]:
            upstream = upstream + ref[...].astype(F32)
        values = hidden_ref[...]
        inverse = lax.rsqrt(jnp.mean(values * values, axis=-1, keepdims=True) + EPS)
        back, terms = normalize_back(values, inverse, gain_ref[...].astype(F32), upstream)
        low_out[...] = (grad_ref[...].astype(F32) + back).astype(BF16)
        terms_out[...] = jnp.sum(terms, axis=0, keepdims=True)

    return call(
        body,
        [array((rows, width), BF16), array((1, width), F32)],
        [kept, hidden, gain, grad_half, *arrived],
    )


def merge_back(own, other, merge_weight, gate_value, attended, places, head_width):
    groups = len(attended)
    half, width = own.shape
    rows = 2 * half
    query_width = attended[0].shape[1]
    per_group = query_width // head_width
    heads = groups * per_group
    middle = width // 2

    def body(at, own_ref, other_ref, w_ref, g_ref, *refs):
        inputs = refs[:groups]
        pieces = refs[groups : 2 * groups]
        hidden_out, core_out, logit_out, stack_s, logit_s = refs[2 * groups :]
        step = pl.program_id(0)

        @pl.when(step == 0)
        def _():
            for place, ref in enumerate(inputs):
                stack_s[place] = ref[...]
            hidden_out[pl.ds(pl.multiple_of(at[groups] * half, half), half), :] = own_ref[...]
            hidden_out[pl.ds(pl.multiple_of((1 - at[groups]) * half, half), half), :] = other_ref[
                ...
            ]
            away = pl.multiple_of((1 - at[groups + 1]) * middle, middle)
            core_out[...] = hidden_out[:, pl.ds(away, middle)]
            logit_s[...] = jnp.zeros(logit_s.shape, F32)

        grad = plain_dot(hidden_out[...], w_ref[...])
        gate = g_ref[...]
        low = (grad * gate).astype(BF16)
        for place in range(groups):

            @pl.when(step == place)
            def _(place=place):
                pieces[place][...] = low

        terms = grad * stack_s[step].astype(F32)
        slope = gate * (1.0 - gate)
        lane = lax.broadcasted_iota(jnp.int32, (rows, heads), 1)
        for h in range(per_group):
            at_head = slice(h * head_width, (h + 1) * head_width)
            column = jnp.sum(terms[:, at_head], axis=1, keepdims=True)
            column = column * slope[:, h * head_width : h * head_width + 1]
            logit_s[...] += jnp.where(lane == at[step] * per_group + h, column, 0.0)

        @pl.when(step == groups - 1)
        def _():
            logit_out[...] = logit_s[...].astype(BF16)

    out = call(
        body,
        [array((rows, query_width), BF16)] * groups
        + [
            array((rows, width), BF16),
            array((rows, middle), BF16),
            array((rows, heads), BF16),
        ],
        [own, other, merge_weight, gate_value, *attended],
        [
            None,
            None,
            pl.BlockSpec((width, query_width), lambda k, at: (0, at[k])),
            pl.BlockSpec((rows, query_width), lambda k, at: (k, 0)),
        ]
        + [None] * groups,
        grid=(groups,),
        scalars=places,
        scratch=[
            pltpu.VMEM((groups, rows, query_width), BF16),
            pltpu.VMEM((rows, heads), F32),
        ],
    )
    return (out[:groups], *out[groups:])


def merge_gradient(hidden_low, hidden_core, gated, gated_core, places, groups):
    rows, width = hidden_low.shape
    wide = gated.shape[1]
    part = width // 4

    def body(at, own_ref, core_ref, gated_ref, gated_core_ref, kept_out, *sent_outs):
        away, piece = 1 - at[groups + 2], part // 2
        for place, begin, size, out in (
            (away, 0, piece, sent_outs[0]),
            (away, piece, piece, sent_outs[1]),
            (at[groups + 2], 0, part, kept_out),
        ):
            first = pl.multiple_of((2 * at[groups + 1] + place) * part + begin, size)
            second = pl.multiple_of(place * part + begin, size)
            value = outer_dot(own_ref[:, pl.ds(first, size)], gated_ref[...])
            value = value + outer_dot(core_ref[:, pl.ds(second, size)], gated_core_ref[...])
            out[...] = value.astype(out.dtype)

    return call(
        body,
        [array((part, wide), F32)] + [array((part // 2, wide), BF16)] * 2,
        [hidden_low, hidden_core, gated, gated_core],
        scalars=places,
    )


def add_split_at(kept, arrived, places):
    parts = places.shape[0]
    rows = kept.shape[0] // parts
    count = len(arrived)

    def body(at, kept_ref, *refs):
        outs, arrived_s = refs[count:-1], refs[-1]
        fill_rows(refs[:count], arrived_s)
        for place, out in enumerate(outs):
            rows_at = pl.ds(pl.multiple_of(at[place] * rows, rows), rows)
            out[...] = (kept_ref[rows_at, :] + arrived_s[rows_at, :].astype(F32)).astype(out.dtype)

    shape = (rows, kept.shape[1])
    out = call(
        body,
        [array(shape, F32)] + [array(shape, BF16)] * (parts - 1),
        [kept, *arrived],
        scalars=places,
        scratch=[pltpu.VMEM(kept.shape, BF16)],
    )
    return (out[0], out[1:])


def input_part(pieces, logits, weights, headgate, places):
    groups = len(pieces)
    rows = pieces[0].shape[0]
    width = headgate.shape[1]
    sizes = [w.shape[0] // groups for w in weights]

    def body(at, q_ref, k_ref, v_ref, h_ref, l_ref, *refs):
        inputs = refs[:groups]
        part_out, stack_s, acc_s = refs[groups:]
        step = pl.program_id(0)

        @pl.when(step == 0)
        def _():
            for place, ref in enumerate(inputs):
                stack_s[place] = ref[...]
            acc_s[...] = plain_dot(l_ref[...], h_ref[...])

        values = stack_s[step]
        total, first = acc_s[...], 0
        for size, ref in zip(sizes, (q_ref, k_ref, v_ref)):
            total = total + plain_dot(values[:, first : first + size], ref[...])
            first += size
        acc_s[...] = total

        @pl.when(step == groups - 1)
        def _():
            part_out[...] = acc_s[...].astype(BF16)

    return call(
        body,
        [array((rows, width), BF16)],
        [*weights, headgate, logits, *pieces],
        [pl.BlockSpec((size, width), lambda k, at: (at[k], 0)) for size in sizes]
        + [None] * (2 + groups),
        grid=(groups,),
        scalars=places,
        scratch=[pltpu.VMEM((groups, rows, sum(sizes)), BF16), pltpu.VMEM((rows, width), F32)],
    )[0]


def input_gradient(part, arrived, tokens, gain, hidden_low):
    rows, width = tokens.shape

    def body(part_ref, arrived_ref, x_ref, gain_ref, hidden_ref, grad_out, terms_out):
        upstream = part_ref[...].astype(F32) + arrived_ref[...].astype(F32)
        values = x_ref[...].astype(F32)
        inverse = lax.rsqrt(jnp.mean(values * values, axis=-1, keepdims=True) + EPS)
        back, terms = normalize_back(values, inverse, gain_ref[...].astype(F32), upstream)
        grad_out[...] = hidden_ref[...].astype(F32) + back
        terms_out[...] = jnp.sum(terms, axis=0, keepdims=True)

    return call(
        body,
        [array((rows, width), F32), array((1, width), F32)],
        [part, arrived, tokens, gain, hidden_low],
    )


def head_gradient(pieces, core_pieces, own_rows, other_rows, places, groups):
    count = len(pieces)
    rows, wide = pieces[0].shape
    half = rows // 2
    middle = other_rows.shape[1]
    part = middle // 2

    def body(at, *refs):
        inputs, core_ref, own_refs = refs[:count], refs[count], refs[count + 1 : 2 * count + 1]
        other_ref, kept_out, sent_out, left_s, right_s = refs[2 * count + 1 :]
        start = 0
        for which in (at[groups], 1 - at[groups]):
            for place, ref in enumerate(inputs):
                own = pl.multiple_of(which * half, half)
                core = pl.multiple_of(which * half + place * rows, half)
                left_s[start : start + half, :] = ref[pl.ds(own, half), :]
                left_s[start + half : start + rows, :] = core_ref[pl.ds(core, half), :]
                start += rows
        fill_rows([*own_refs, other_ref], right_s)
        left = left_s[...]
        for place, out in ((1 - at[groups + 2], sent_out), (at[groups + 2], kept_out)):
            columns = pl.ds(pl.multiple_of(place * part, part), part)
            out[...] = outer_dot(left, right_s[:, columns], out.dtype)

    return call(
        body,
        [array((wide, part), F32), array((wide, part), BF16)],
        [*pieces, core_pieces, *own_rows, other_rows],
        scalars=places,
        scratch=[
            pltpu.VMEM((2 * count * rows, wide), BF16),
            pltpu.VMEM((2 * count * rows, middle), BF16),
        ],
    )


def add_columns_at(kept, arrived, places):
    rows, width = kept.shape
    middle = width // 2

    def body(at, kept_ref, arrived_ref, kept_out, sent_out):
        for place, out in enumerate((kept_out, sent_out)):
            columns = pl.ds(pl.multiple_of(at[place] * middle, middle), middle)
            out[...] = (kept_ref[:, columns] + arrived_ref[:, columns].astype(F32)).astype(
                out.dtype
            )

    return call(
        body,
        [array((rows, middle), F32), array((rows, middle), BF16)],
        [kept, arrived],
        scalars=places,
    )


def assemble(parts, order, heights, row_blocks, column_blocks, before=()):
    count = order.shape[0] // 2
    wide = parts[0].shape[1]
    tall = sum(heights)
    rows = sum(part.shape[0] for part in parts)
    assert rows == count * tall
    begins = [sum(heights[:i]) for i in range(len(heights))]

    def body(at, *refs):
        inputs = refs[: len(parts)]
        outs = refs[len(parts) + len(before) : len(parts) + len(before) + len(heights)]
        values_s, sems = refs[-2:]
        copies, start = [], 0
        for ref in inputs:
            for first in range(0, ref.shape[0], tall):
                block = start // tall
                values_s[start : start + tall, :] = ref[first : first + tall, :].astype(F32)
                for which, (height, begin, out) in enumerate(zip(heights, begins, outs)):
                    row = pl.multiple_of(at[block] * height, height)
                    column = pl.multiple_of(at[count + block] * wide, wide)
                    copy = pltpu.make_async_copy(
                        values_s.at[pl.ds(start + begin, height), :],
                        out.at[pl.ds(row, height), pl.ds(column, wide)],
                        sems.at[block, which],
                    )
                    copy.start()
                    copies.append(copy)
                start += tall
        for copy in copies:
            copy.wait()

    return pl.pallas_call(
        body,
        out_shape=[
            array((height * row_blocks, wide * column_blocks), F32) for height in heights
        ],
        grid_spec=pltpu.PrefetchScalarGridSpec(
            num_scalar_prefetch=1,
            grid=(1,),
            in_specs=[whole(part) for part in parts] + anywhere(before),
            out_specs=anywhere(heights),
            scratch_shapes=[
                pltpu.VMEM((rows, wide), F32),
                pltpu.SemaphoreType.DMA((count, len(heights))),
            ],
        ),
        input_output_aliases={1 + len(parts) + i: i for i in range(len(before))},
        cost_estimate=pl.CostEstimate(flops=0, bytes_accessed=1024, transcendentals=0),
        compiler_params=pltpu.CompilerParams(vmem_limit_bytes=60 * 1024 * 1024),
    )(order, *parts, *before)


def shards(
    tokens,
    item_lengths,
    first_gain,
    query_weight,
    key_weight,
    value_weight,
    headgate_weight,
    merge_weight,
    query_norm,
    key_norm,
    second_gain,
    gate_weight,
    up_weight,
    down_weight,
    out_cotangent,
):
    sp_size = lax.axis_size("sp")
    device = lax.axis_index("sp")
    side = lax.axis_index("tp")
    local_rows, width = tokens.shape
    half_rows = local_rows // 2
    head_width = query_norm.shape[0]
    local_heads = query_weight.shape[0] // head_width
    groups = key_weight.shape[0] // head_width
    query_width = local_heads // groups * head_width
    score_scale = 1.0 / math.sqrt(head_width)

    bits = sp_size.bit_length() - 1
    group_step = 1 << (bits // 2)
    group_masks = [group_step * k for k in range(1, groups)]
    all_group_masks = [0] + group_masks
    group_bits = group_step * (groups - 1)
    rest = [1 << b for b in range(1, bits) if not (1 << b) & group_bits] + [1]
    rest_count = 1 << len(rest)
    rest_masks = [
        sum(mask for b, mask in enumerate(rest) if r >> b & 1) for r in range(rest_count)
    ]
    row_masks = rest[:-1]
    order = [outer ^ mask for outer in rest_masks for mask in all_group_masks]
    own_group = (device // group_step) % groups
    own_rest = sum(((device // mask) % 2) * (1 << b) for b, mask in enumerate(rest))
    group_places = own_group ^ jnp.arange(groups, dtype=jnp.int32)
    rest_places = own_rest ^ jnp.arange(rest_count, dtype=jnp.int32)
    rest_bits = [(own_rest >> b) & 1 for b in range(len(rest))]
    places = jnp.concatenate(
        [group_places, jnp.stack([side, rest_bits[-1], rest_bits[-2]]).astype(jnp.int32)]
    )

    def level(b):
        return jnp.stack([rest_bits[b], 1 - rest_bits[b]]).astype(jnp.int32)

    device_order = device ^ jnp.array(order, dtype=jnp.int32)

    def across_groups(pieces):
        return [pieces[0]] + [exchange(p, mask) for p, mask in zip(pieces[1:], group_masks)]

    def row_groups(values):
        return [values] + [exchange(values, mask) for mask in group_masks]

    def row_pieces(pieces, *others):
        pieces = list(pieces)
        for mask in row_masks:
            pieces.append(exchange(after(stack_rows(*pieces), *others), mask))
        return pieces

    def add_rows(kept, arrived):
        for mask in reversed(row_masks[:-1]):
            kept, (sent,) = add_split(kept, arrived, 2)
            arrived = exchange(sent, mask)
        return add_split(kept, arrived, groups)

    first_gain_row = first_gain.reshape(1, width)
    second_gain_row = second_gain.reshape(1, width)
    query_gain = query_norm.astype(F32).reshape(1, head_width)
    key_gain = key_norm.astype(F32).reshape(1, head_width)

    projections = (query_weight, key_weight, value_weight)
    sent, normed_low, normed_half, normed_core, grad_half, gate_value = project(
        tokens,
        first_gain_row,
        projections,
        headgate_weight,
        out_cotangent,
        places,
        groups,
    )
    raw = across_groups(sent)
    own_stack = after(stack_rows(gate_weight, up_weight, down_weight), *sent)
    side_stack = swap(own_stack)
    core_stack = exchange(own_stack, 1)
    raw = after_all(raw, core_stack)

    item = jnp.arange(item_lengths.shape[0], dtype=jnp.int32)
    item_starts = jnp.sum(
        jnp.where(item[:, None] < item[None, :], item_lengths[:, None], 0), axis=0
    )
    within = jnp.arange(local_rows, dtype=jnp.int32)
    row_devices = device ^ jnp.array(all_group_masks, dtype=jnp.int32)
    row_index = (row_devices[:, None] * local_rows + within[None, :]).reshape(-1, 1)
    key_index = (device_order[:, None] * local_rows + within[None, :]).reshape(1, -1)
    begins = jnp.max(
        jnp.where(item_starts[None, :] <= row_index, item_starts[None, :], 0),
        axis=1,
        keepdims=True,
    )
    lane = jnp.arange(head_width, dtype=jnp.int32)
    frequency = THETA ** (
        -2.0 * (lane % (head_width // 2)).astype(F32) / head_width
    )
    angles = (row_index - begins).astype(F32) * frequency[None, :]
    cosine = jnp.cos(angles)
    sine = jnp.sin(angles) * jnp.where(lane < head_width // 2, -1.0, 1.0)

    bounds = jnp.concatenate([item_starts, row_devices * local_rows]).astype(jnp.int32)
    queries, pair_own = head_forward(raw, cosine, sine, query_gain, key_gain)
    grad_groups = row_groups(after(grad_half, pair_own))
    pairs = [pair_own]
    for mask in rest:
        pairs.append(exchange(pairs[0] if len(pairs) == 1 else stack_rows(*pairs), mask))
    attended, log_sums, attended_low = attend(
        queries, pairs, key_index, bounds, groups, score_scale
    )
    attended_rows = across_groups(after_all(attended_low, *grad_groups))
    attended_rows = after_all(attended_rows, side_stack)
    side_core_stack = exchange(after(side_stack, *attended_rows), 1)
    gated_low, sent, kept = merge(attended_rows, gate_value, merge_weight, tokens, places)
    normed_side = stack_rows(normed_half, exchange(after(normed_core, *attended_rows), 1))
    arrived = after(swap(sent), side_core_stack, normed_side)
    gated_core = exchange(gated_low, 1)
    hidden, second_low = second_norm(kept, arrived, second_gain_row)

    stacks = [own_stack, side_stack, core_stack, side_core_stack]
    second_groups = row_groups(second_low)
    grads_low, grad_act = act_gradient(row_pieces(grad_groups, *attended_low), stacks)
    inputs = row_pieces(second_groups, grads_low, gated_core)
    side_rows = row_groups(after(normed_side, *second_groups))
    near = feed(inputs[:-1], grad_act, stacks, 0, F32)
    far_inputs = after_all(inputs[-1:], near[2], *side_rows)
    far = feed(far_inputs, grad_act, stacks, 1, BF16)
    (near_low, near_left, kept), (far_low, far_left, sent) = near, far
    lefts = [near_left, far_left]
    arrived = exchange(sent, row_masks[-1])
    other_rows = swap(after(stack_rows(*side_rows), sent))
    branch_kept, branch_sent = branch(lefts, stacks)
    unit_kept, unit_sent = unit_gradients(lefts, [near_low, far_low], grads_low)
    kept, sent = add_rows(after(kept, branch_sent, unit_sent, other_rows), arrived)
    branch_arrived = exchange(after(branch_sent, kept), row_masks[-1])
    unit_arrived = exchange(after(unit_sent, kept), 1)
    arrived = [exchange(piece, mask) for piece, mask in zip(sent, group_masks)]
    unit_own, unit_sent = add_units(unit_kept, unit_arrived)
    hidden_half, second_terms = hidden_gradient(
        after(kept, unit_own), arrived, hidden, second_gain_row, grad_half
    )
    branch_kept, branch_sent = add_rows(branch_kept, branch_arrived)
    branch_first = exchange(branch_sent[0], group_masks[0])
    hidden_other = after(swap(hidden_half), *branch_sent)
    grad_pieces, hidden_low, hidden_core, grad_logit_low = merge_back(
        hidden_half, hidden_other, merge_weight, gate_value, attended_rows, places, head_width
    )

    grad_grouped = across_groups(after_all(grad_pieces, branch_first))
    merge_kept, *merge_sent = merge_gradient(
        hidden_low, exchange(hidden_core, 1), gated_low, gated_core, places, groups
    )
    merge_first = exchange(merge_sent[0], rest[-2])

    grad_grouped = after_all(grad_grouped, merge_kept)
    branch_second = exchange(after(branch_sent[1], *grad_grouped), group_masks[1])
    grad_queries, kept, sent = attend_back(
        queries,
        pairs,
        key_index,
        bounds,
        grad_grouped,
        attended,
        log_sums,
        score_scale,
    )
    sent = after(sent, branch_second, merge_first)
    for mask in reversed(rest[1:]):
        kept, (sent,) = add_split(kept, exchange(sent, mask), 2)
    branch_third = [
        exchange(after(piece, branch_second), mask)
        for piece, mask in zip(branch_sent[2:], group_masks[2:])
    ]
    branch_arrived = [branch_first, branch_second, *branch_third]
    arrived = exchange(sent, rest[0])
    merge_second = exchange(after(merge_sent[1], arrived), rest[-2])
    head_grads, head_stack, head_gains = head_backward(
        raw, cosine, sine, query_gain, key_gain, grad_queries, kept, arrived
    )
    head_core = exchange(head_stack, 1)

    back = across_groups(after_all(head_grads, *branch_arrived, head_core))
    part = input_part(back, grad_logit_low, projections, headgate_weight, places)
    part_other = swap(part)
    input_grad, first_terms = input_gradient(
        part, part_other, tokens, first_gain_row, hidden_low
    )
    kept, sent = head_gradient(head_grads, head_core, side_rows, other_rows, places, groups)
    arrived = exchange(after(sent, merge_second), rest[-2])
    for b in reversed(range(len(rest) - 2)):
        kept, sent = add_columns_at(kept, arrived, level(b))
        arrived = exchange(sent, rest[b])
    head_block = (kept + arrived.astype(F32)).astype(BF16)
    merge_arrived = [merge_first, merge_second]
    for b in reversed(range(len(rest) - 2)):
        merge_kept, (merge_sent,) = add_split_at(merge_kept, merge_arrived, level(b))
        merge_arrived = [exchange(merge_sent, rest[b])]

    merge_kept, merge_sent = add_split_at(merge_kept, merge_arrived, group_places)
    merge_sent = after_all(merge_sent, *back)
    merge_arrived = [exchange(piece, mask) for piece, mask in zip(merge_sent, group_masks)]
    unit_side = swap(after(unit_sent, part_other))
    query_block, key_block, value_block = (
        head_block[:query_width],
        head_block[query_width : query_width + head_width],
        head_block[query_width + head_width :],
    )

    def all_parts(pieces, *others):
        parts = [stack_rows(*pieces)]
        for mask in row_masks:
            parts = parts + [exchange(after(part, *others), mask) for part in parts]
        return parts

    def core_parts(parts, *others):
        return [exchange(after(part, *others), 1) for part in parts]

    query_groups = row_groups(after(query_block, *merge_arrived))
    merge_block = merge_kept
    for piece in merge_arrived:
        merge_block = merge_block + piece.astype(F32)
    merge_groups = row_groups(after(merge_block.astype(BF16), *query_groups))
    query_parts = all_parts(query_groups)
    key_groups = row_groups(after(key_block, unit_side, *merge_groups, *query_parts))
    merge_parts = all_parts(merge_groups)
    query_core = core_parts(query_parts, *merge_groups)
    value_groups = row_groups(after(value_block, *key_groups, *merge_parts, *query_core))
    key_parts = all_parts(key_groups)
    merge_core = core_parts(merge_parts, *key_groups)
    value_parts = all_parts(after_all(value_groups, *key_parts, *merge_core))
    key_core = core_parts(key_parts)

    block_rows = jnp.tile(group_places, rest_count)
    block_columns = jnp.repeat(rest_places, groups)
    strips = block_columns * groups + block_rows
    block_order = jnp.concatenate([block_rows, block_columns])
    (query_grad,) = assemble(
        [*query_parts, *query_core], block_order, (query_width,), groups, rest_count
    )
    (merge_grad,) = assemble(
        [*merge_parts, *merge_core],
        jnp.concatenate([strips, jnp.zeros_like(strips)]),
        (width // sp_size,),
        sp_size,
        1,
    )
    (key_grad,) = assemble(
        [*key_parts, *key_core], block_order, (head_width,), groups, rest_count
    )
    value_core = core_parts(value_parts, query_grad, merge_grad, key_grad)
    (value_grad,) = assemble(
        [*value_parts, *value_core], block_order, (head_width,), groups, rest_count
    )

    for piece in branch_arrived:
        branch_kept = branch_kept + piece.astype(F32)
    output_half = (hidden + branch_kept).astype(BF16)
    output_other = swap(output_half)
    layer_output = jnp.where(
        side == 0,
        stack_rows(output_half, output_other),
        stack_rows(output_other, output_half),
    )
    unit_sum = unit_own + unit_side.astype(F32)
    units = gate_weight.shape[0]
    gate_acc, up_acc, down_acc = (unit_sum[i * units : (i + 1) * units] for i in range(3))

    headgate_part = outer_dot(grad_logit_low, normed_low)
    gains = jnp.concatenate(
        [head_gains[0], head_gains[1], jnp.zeros((width - 2 * head_width,), F32)]
    )
    sides = stack_rows(second_terms, gains[None])
    sides = sides + swap(sides)
    small = after(stack_rows(headgate_part, first_terms, sides), *merge_arrived)
    for mask in rest:
        small = small + exchange(small, mask)
    small = after(small, *value_groups)
    small = small + sum(exchange(small, mask) for mask in group_masks)

    return (
        layer_output,
        input_grad,
        small[local_heads],
        query_grad,
        key_grad,
        value_grad,
        small[:local_heads],
        merge_grad,
        small[local_heads + 2, :head_width],
        small[local_heads + 2, head_width : 2 * head_width],
        small[local_heads + 1],
        gate_acc,
        up_acc,
        down_acc,
    )


def solution(mesh):
    return jax.shard_map(
        shards,
        mesh=mesh,
        in_specs=(
            P("sp", None),
            P(),
            P(),
            P("tp", None),
            P("tp", None),
            P("tp", None),
            P("tp", None),
            P(None, "tp"),
            P(),
            P(),
            P(),
            P(("tp", "sp"), None),
            P(("tp", "sp"), None),
            P(("tp", "sp"), None),
            P("sp", None),
        ),
        out_specs=(
            P("sp", None),
            P("sp", None),
            P(),
            P("tp", None),
            P("tp", None),
            P("tp", None),
            P("tp", None),
            P(None, "tp"),
            P(),
            P(),
            P(),
            P(("tp", "sp"), None),
            P(("tp", "sp"), None),
            P(("tp", "sp"), None),
        ),
        check_vma=False,
    )
```
